256 devices in a mesh: obs: 64 (over z, x, core), sub: 4 (over y).
Axes of the slice: x: 4, y: 4, z: 8, core: 2. Of those that a mesh axis runs over, the one named last changes fastest.
Arguments:
- jacobian: bfloat16 [262144, 2048], P(('obs', 'sub')), may hold values from -0.09375 to 0.09375
- obs_weight: float32 [262144], P(('obs', 'sub')), may hold values from 0.2 to 5
- row_counts: int32 [64], P('obs'), may hold values from 1 to 4096, 196608 in all
- tile_lists: int32 [64, 8], replicated, may hold values from 0 to 15, all different within a row
- tile_slot: int32 [16], replicated, may hold values from 0 to 15, each once
- probe_block: bfloat16 [4096, 256], P('obs'), may hold values from -6 to 6
Outputs:
- owned_product: bfloat16 [4096, 256], P('obs', 'sub')
The draws below stay inside these ranges and needn't reach their ends.
Inputs may be any that keep to these rules, and one draw needn't show every extreme that they name: `row_counts`: the live counts of one block; some block is full (4096) in every draw. `tile_lists`: each row lists 8 different tiles; every tile is listed by some block. `tile_slot`: a permutation of the tiles.
All inputs are finite; a program needn't handle non-finite values.
Results may differ from the reference program's by a relative error of at most 0.0034.
Values may be sent and summed in bfloat16 or wider, within the bound.
A program may use at most 64 MiB of HBM per device.

```python
import math
import jax
import jax.numpy as jnp
import numpy as np
from jax import lax

TILE = 256
PROBE = 256
KT = 8
NT = 16
ROWS = 1024
BLOCK = 4096
KC = 2048
OBS_ALL = 262144
N_OBS = 64


def level_of(stream_key, shape, split, least, top_value):
    def one(axis_at, parts):
        steps = jax.random.uniform(jax.random.fold_in(jax.random.fold_in(stream_key, 6), axis_at), (parts,), jnp.float32, least / len(split), top_value / len(split))
        return jnp.repeat(jnp.exp(steps), shape[axis_at] // parts).reshape((-1,) + (1,) * (len(shape) - axis_at - 1))

    loudness = one(*split[0])
    for cut in split[1:]:
        loudness = loudness * one(*cut)
    return loudness


def choose_distinct(key, rows, count, top, lift):
    order = jax.random.permutation(jax.random.fold_in(key, 1), count)
    favour = order
    for power in range(3):
        favour = favour * favour // count
    favour = favour * lift // count
    chance = jax.random.randint(jax.random.fold_in(key, 2), (rows, count), 0, 4096) + favour
    sure = jax.random.permutation(jax.random.fold_in(key, 3), rows)[jnp.arange(count) % rows]
    chance = jnp.where(jnp.arange(rows)[:, None] == sure[None, :], 1 << 14, chance)
    score = chance * count + jnp.arange(count)
    return lax.top_k(score.astype(jnp.int32), top)[1].astype(jnp.int32)


def length_profile(count, total, bound, slope):
    weights = [(1 << 20) // math.isqrt(grade ** slope) + 1 for grade in range(2, count + 1)]
    spare, given = total - bound - (count - 1), [1] * (count - 1)
    while spare > 0:
        candidates = [i for i in range(count - 1) if given[i] < bound]
        pool, budget = sum([weights[i] for i in candidates]), spare
        for i in candidates:
            extra = min(bound - given[i], max(1, budget * weights[i] // pool), spare)
            given[i] = given[i] + extra
            spare = spare - extra
    return np.array([bound] + given)


def ragged_sizes(stream_key, number_of, total, limit, lean):
    if number_of == 2:
        one = jax.random.randint(stream_key, (), max(1, total - limit), min(limit, total - 1) + 1)
        return jnp.stack([one, total - one])
    lengths = jnp.asarray(length_profile(number_of, total, limit, lean), jnp.int32)
    twos = (number_of - 1) // 2
    source_of, receiver = lengths[1:1 + 2 * twos:2], lengths[2:2 + 2 * twos:2]
    slack = jnp.minimum(source_of - 1, limit - receiver)
    shifted = jax.random.randint(jax.random.fold_in(stream_key, 1), (twos,), 0, 1 << 20) % (slack + 1)
    lengths = lengths.at[1:1 + 2 * twos:2].set(source_of - shifted).at[2:2 + 2 * twos:2].set(receiver + shifted)
    return lengths[jax.random.permutation(jax.random.fold_in(stream_key, 2), number_of)]


def normal_values(own_key, dims, spread, reach, split=(), held_as=jnp.bfloat16):
    loudness = level_of(own_key, dims, split, -0.22, 0.18) if split else 1.0
    values = jax.random.normal(own_key, dims, jnp.float32) * spread * loudness
    return jnp.minimum(jnp.maximum(values, -reach), reach).astype(held_as)


def setup_inputs(seed: int = 0) -> dict:
    streams_of = jax.random.split(jax.random.key(seed), 7)
    return {
        "jacobian": normal_values(streams_of[0], (OBS_ALL, KC), BLOCK ** -0.5, 0.09375, ((0, 256),)),
        "obs_weight": jnp.clip(jnp.exp(math.log(5.0) - 3.218876 * jax.random.uniform(streams_of[1], (OBS_ALL,), jnp.float32) ** level_of(streams_of[1], (OBS_ALL,), ((0, 256),), -0.2, 0.2)), 0.2, 5.0),
        "row_counts": ragged_sizes(streams_of[2], N_OBS, 3 * N_OBS * ROWS, BLOCK, 2).astype(jnp.int32),
        "tile_lists": choose_distinct(streams_of[3], N_OBS, NT, KT, 8192),
        "tile_slot": jax.random.permutation(streams_of[4], NT).astype(jnp.int32),
        "probe_block": normal_values(streams_of[5], (NT * TILE, PROBE), 1.0, 6.0, ((0, 64),)),
    }


def reference(jacobian, obs_weight, row_counts, tile_lists, tile_slot, probe_block):
    blocks = jacobian.reshape(N_OBS, BLOCK, KC)
    weights = obs_weight.reshape(N_OBS, BLOCK)
    probe_tiles = probe_block.reshape(NT, TILE, PROBE)

    def one_block(inputs):
        jac_block, weight_block, count, columns = inputs
        live = (jnp.arange(BLOCK, dtype=jnp.int32) < count).astype(jnp.float32)
        weighted = (jac_block.astype(jnp.float32) * (weight_block * live)[:, None]).astype(jnp.bfloat16)
        probe_cols = probe_tiles[columns.astype(jnp.int32)].reshape(KC, PROBE)
        image = jnp.dot(jac_block, probe_cols, preferred_element_type=jnp.float32).astype(jnp.bfloat16)
        contrib = lax.dot_general(weighted, image, (((0,), (0,)), ((), ())),
                                  preferred_element_type=jnp.float32)
        return contrib.reshape(KT, TILE, PROBE)

    contribs = lax.map(one_block, (blocks, weights, row_counts, tile_lists))
    product = jnp.zeros((NT, TILE, PROBE), jnp.float32)
    product = product.at[tile_lists.reshape(-1).astype(jnp.int32)].add(
        contribs.reshape(N_OBS * KT, TILE, PROBE).astype(jnp.float32))
    placed = jnp.zeros((NT, TILE, PROBE), jnp.float32).at[tile_slot.astype(jnp.int32)].set(product)
    return placed.reshape(NT * TILE, PROBE).astype(jnp.bfloat16)
```

```python
import jax
import jax.numpy as jnp
from jax import lax
from jax.experimental import pallas as pl
from jax.experimental.pallas import tpu as pltpu
from jax.sharding import PartitionSpec as P

MESH = pl.DeviceIdType.MESH
X, Y, Z = 4, 4, 8
F32, BF16 = jnp.float32, jnp.bfloat16

STAGES = 3


def kernel(lists_ref, slot_ref, count_ref, w_ref, jac_ref, probe_ref, out_ref,
           table, pb, jv, g, img, cown, csend, crecv, d, ra, rb, rc, e, r3, fin,
           s_loc, s_jac, s_a, r_a, s_b, r_b, s_ring, r_ring, s_p, r_p, s_c, r_c,
           s_q, r_q, s_z, r_z):
    obs, y = lax.axis_index("obs"), lax.axis_index("sub")
    c = obs % 2
    x = (obs // 2) % X
    z = obs // (2 * X)

    def dev(zz, xx, cc, yy=None):
        return ((zz * X + xx) * 2 + cc, y if yy is None else yy)

    def send(src, dst, s, r, to):
        copy = pltpu.make_async_remote_copy(src_ref=src, dst_ref=dst, send_sem=s, recv_sem=r, device_id=to, device_id_type=MESH)
        copy.start()
        return copy

    def arrived(dst, r):
        pltpu.make_async_remote_copy(src_ref=dst, dst_ref=dst, send_sem=s_loc.at[2], recv_sem=r, device_id=dev(z, x, 1 - c),
                                     device_id_type=MESH).wait_recv()

    def sent(src, s):
        pltpu.make_async_remote_copy(src_ref=src, dst_ref=src, send_sem=s, recv_sem=s_loc.at[2], device_id=dev(z, x, 1 - c),
                                     device_id_type=MESH).wait_send()

    partner = dev(z, x, 1 - c)
    pltpu.make_async_copy(probe_ref, pb, s_loc.at[0]).start()
    for k in range(8):
        pltpu.make_async_copy(jac_ref.at[:, pl.ds(k * 256, 256)], jv.at[k], s_jac.at[k]).start()

    barrier = pltpu.get_barrier_semaphore()
    others = [(z, (x + dx) % X, cc, y) for dx in range(1, X) for cc in range(2)]
    others += [((z + dz) % Z, x, cc, y) for dz in range(1, Z) for cc in range(2)]
    others += [(z, x, 1 - c, y), (z, x, c, (y + 1) % Y), (z, x, c, (y + Y - 1) % Y)]
    for o in others:
        pl.semaphore_signal(barrier, inc=1, device_id=dev(*o), device_id_type=MESH)

    def fill(t, _):
        for which, owner in enumerate((obs, obs + 1 - 2 * c)):
            at, found = jnp.int32(0), jnp.int32(0)
            for k in range(8):
                hit = slot_ref[lists_ref[k, owner]] == t
                at = jnp.where(hit, k, at)
                found = jnp.where(hit, 1, found)
            table[2 * which, t] = at
            table[2 * which + 1, t] = found
        return 0

    lax.fori_loop(0, 16, fill, 0)
    pltpu.make_async_copy(probe_ref, pb, s_loc.at[0]).wait()
    pl.semaphore_wait(barrier, len(others))

    half0, half1 = pb.at[:, pl.ds(0, 128)], pb.at[:, pl.ds(128, 128)]
    mine0 = g.at[0, z, x, pl.ds(c * 64, 64)]
    mine1 = g.at[1, z, x, pl.ds(c * 64, 64)]

    @pl.when(c == 0)
    def _():
        pltpu.make_async_copy(half0, mine0, s_loc.at[1]).start()
        send(half1, mine1, s_b.at[0], r_b.at[z * 2], partner)

    @pl.when(c == 1)
    def _():
        send(half0, mine0, s_a.at[0], r_a.at[x * 2 + 1], partner)
        pltpu.make_async_copy(half1, mine1, s_loc.at[1]).start()

    for dx in (1, 3, 2):
        send(half0, mine0, s_a.at[dx], r_a.at[x * 2 + c], dev(z, (x + dx) % X, 0))
    for dz in (4, 3, 5, 2, 6, 1, 7):
        send(half1, mine1, s_b.at[dz], r_b.at[z * 2 + c], dev((z + dz) % Z, x, 1))

    def piece0(zz, xx):
        return g.at[0, zz, xx]

    @pl.when(c == 0)
    def _():
        n = 0
        for i, dx in enumerate((0, 1, 3, 2)):
            xx = (x + dx) % X
            for cc in range(2):
                if dx == 0 and cc == 0:
                    pltpu.make_async_copy(half0, mine0, s_loc.at[1]).wait()
                else:
                    arrived(g.at[0, z, xx, pl.ds(cc * 64, 64)], r_a.at[xx * 2 + cc])
            for way, to in ((0, (z + 1) % Z), (1, (z + Z - 1) % Z)):
                send(piece0(z, xx), piece0(z, xx), s_ring.at[way, i], r_ring.at[way, i], dev(to, x, 0))
            send(piece0(z, xx), piece0(z, xx), s_p.at[n], r_p.at[n], partner)
            n += 1
        for step in range(1, 5):
            for i, dx in enumerate((0, 1, 3, 2)):
                xx = (x + dx) % X
                for way in range(2):
                    if step == 4 and way != i // 2:
                        continue
                    zz = (z + Z - step) % Z if way == 0 else (z + step) % Z
                    to = (z + 1) % Z if way == 0 else (z + Z - 1) % Z
                    q = piece0(zz, xx)
                    arrived(q, r_ring.at[way, (step - 1) * 4 + i])
                    if step < 3 or (step == 3 and way == i // 2):
                        send(q, q, s_ring.at[way, step * 4 + i], r_ring.at[way, step * 4 + i], dev(to, x, 0))
                    send(q, q, s_p.at[n], r_p.at[n], partner)
                    n += 1

    near = (0, 1, 7, 2, 6, 3, 5, 4)

    @pl.when(c == 1)
    def _():
        n = 0
        for i, dz in enumerate(near):
            zz = (z + dz) % Z
            for cc in range(2):
                if dz == 0 and cc == 1:
                    pltpu.make_async_copy(half1, mine1, s_loc.at[1]).wait()
                else:
                    arrived(g.at[1, zz, x, pl.ds(cc * 64, 64)], r_b.at[zz * 2 + cc])
            q = g.at[1, zz, x]
            for way, to in ((0, (x + 1) % X), (1, (x + X - 1) % X)):
                send(q, q, s_ring.at[way, i], r_ring.at[way, i], dev(z, to, 1))
            send(q, q, s_p.at[n], r_p.at[n], partner)
            n += 1
        for step in range(1, 3):
            for i, dz in enumerate(near):
                zz = (z + dz) % Z
                for way in range(2):
                    if step == 2 and way != i % 2:
                        continue
                    xx = (x + X - step) % X if way == 0 else (x + step) % X
                    to = (x + 1) % X if way == 0 else (x + X - 1) % X
                    q = g.at[1, zz, xx]
                    arrived(q, r_ring.at[way, (step - 1) * 8 + i])
                    if step == 1 and way == i % 2:
                        send(q, q, s_ring.at[way, step * 8 + i], r_ring.at[way, step * 8 + i], dev(z, to, 1))
                    send(q, q, s_p.at[n], r_p.at[n], partner)
                    n += 1

    for n in range(32):
        arrived(g.at[0, 0, 0], r_p.at[n])

    for k in range(8):
        pltpu.make_async_copy(jac_ref.at[:, pl.ds(k * 256, 256)], jv.at[k], s_jac.at[k]).wait()

    def image(i, _):
        rows = pl.ds(pl.multiple_of(i * 256, 256), 256)
        total = jnp.zeros((256, 256), F32)
        for k in range(8):
            t = lists_ref[k, obs]
            cols = jnp.concatenate([g[h, t // 2, pl.ds((t % 2) * 2, 2)].reshape(256, 128) for h in range(2)], axis=1)
            total += jnp.dot(jv[k, rows, :], cols, preferred_element_type=F32)
        turned = total.T
        for j in range(2):
            lane = lax.broadcasted_iota(jnp.int32, (1, 128), 1) + (y * 1024 + (i * 2 + j) * 128)
            weight = jnp.where(lane < count_ref[0], w_ref[pl.ds(i * 2 + j, 1), :], 0.0)
            img[:, pl.ds(pl.multiple_of(i * 256 + j * 128, 128), 128)] = (turned[:, j * 128:(j + 1) * 128] * weight).astype(BF16)
        return 0

    lax.fori_loop(0, 4, image, 0)

    low = lax.broadcasted_iota(jnp.int32, (1, 1, 128), 2) < 64

    def contribution(k, _):
        total = jnp.dot(img[...], jv[k], preferred_element_type=F32).reshape(4, 2, 32, 256)
        for b in range(2):
            up = total[:, 0, :, b * 128:(b + 1) * 128]
            down = total[:, 1, :, b * 128:(b + 1) * 128]
            first = jnp.where(low, up, pltpu.roll(down, 64, 2))
            second = jnp.where(low, pltpu.roll(up, 64, 2), down)
            cown[k, b] = jnp.where(c == 0, first, second)
            csend[k, b] = jnp.where(c == 0, second, first).astype(BF16)
        send(csend.at[k], crecv.at[k], s_c.at[k], r_c.at[k], partner)
        return 0

    lax.fori_loop(0, 8, contribution, 0)
    for k in range(8):
        arrived(crecv.at[k], r_c.at[k])

    def place(t, _):
        mine = cown[table[0, t]] * table[1, t].astype(F32)
        other = crecv[table[2, t]].astype(F32) * table[3, t].astype(F32)
        both = (mine + other).astype(BF16)
        for b in range(2):
            xx = 2 * (t % 2) + b
            for yy in range(4):
                d[jnp.where(c == 0, yy, xx), jnp.where(c == 0, xx, yy), t // 2] = both[b, yy]
        return 0

    lax.fori_loop(0, 16, place, 0)

    def along(axis, by):
        if axis == 0:
            return ((z * X + jnp.where(c == 0, x, (x + by) % X)) * 2 + c, jnp.where(c == 0, (y + by) % Y, y))
        return ((z * X + jnp.where(c == 0, (x + by) % X, x)) * 2 + c, jnp.where(c == 0, y, (y + by) % Y))

    def ring(axis, buf, here, lo, hi, ra, rb, rc):
        nxt, opp, prv = (here + 1) % 4, (here + 2) % 4, (here + 3) % 4
        right, left = along(axis, 1), along(axis, 3)
        o = axis * 6
        started = [
            send(buf.at[opp, lo], ra.at[0], s_q.at[o], r_q.at[o], right),
            send(buf.at[opp, hi], ra.at[1], s_q.at[o + 1], r_q.at[o + 1], left),
            send(buf.at[nxt, hi], rb.at[0], s_q.at[o + 2], r_q.at[o + 2], right),
            send(buf.at[prv, lo], rb.at[1], s_q.at[o + 3], r_q.at[o + 3], left),
        ]
        for i, (to, part, dst) in enumerate(((nxt, lo, right), (prv, hi, left))):
            arrived(ra.at[i], r_q.at[o + i])
            buf[to, part] = (buf[to, part].astype(F32) + ra[i].astype(F32)).astype(BF16)
            started.append(send(buf.at[to, part], rc.at[i], s_q.at[o + 4 + i], r_q.at[o + 4 + i], dst))
        arrived(rb.at[1], r_q.at[o + 3])
        arrived(rb.at[0], r_q.at[o + 2])
        arrived(rc.at[0], r_q.at[o + 4])
        arrived(rc.at[1], r_q.at[o + 5])
        return started

    first_here = jnp.where(c == 0, y, x)
    second_here = jnp.where(c == 0, x, y)
    lo, hi = pl.ds(0, 2), pl.ds(2, 2)
    started = ring(0, d, first_here, lo, hi, ra, rb, rc)
    e[lo] = (d[first_here, lo].astype(F32) + rc[0].astype(F32) + rb[1].astype(F32)).astype(BF16)
    e[hi] = (d[first_here, hi].astype(F32) + rb[0].astype(F32) + rc[1].astype(F32)).astype(BF16)

    lo, hi = pl.ds(0, 4), pl.ds(4, 4)
    ra2, rb2, rc2 = [r3.at[pl.ds(n * 2, 2)] for n in range(3)]
    started += ring(1, e, second_here, lo, hi, ra2, rb2, rc2)
    fin[lo] = e[second_here, lo].astype(F32) + rc2[0].astype(F32) + rb2[1].astype(F32)
    fin[hi] = e[second_here, hi].astype(F32) + rb2[0].astype(F32) + rc2[1].astype(F32)

    for dz in (4, 3, 5, 2, 6, 1, 7):
        started.append(send(fin.at[(z + dz) % Z], fin.at[8 + dz], s_z.at[dz], r_z.at[dz], dev((z + dz) % Z, x, c)))
    total = fin[z]
    for dz in (1, 7, 2, 6, 3, 5, 4):
        arrived(fin.at[8 + dz], r_z.at[dz])
        total = total + fin[8 + dz]
    turned = total.T
    out_ref[:, 0:32] = turned[0:64].astype(BF16)
    out_ref[:, 32:64] = turned[64:128].astype(BF16)

    for copy in started:
        copy.wait_send()
    for k in range(8):
        sent(csend.at[k], s_c.at[k])
    for dx in (1, 3, 2):
        sent(half0, s_a.at[dx])
    for dz in range(1, 8):
        sent(half1, s_b.at[dz])
    for n in range(32):
        sent(g.at[0, 0, 0], s_p.at[n])

    @pl.when(c == 0)
    def _():
        sent(half1, s_b.at[0])
        for way in range(2):
            for n in range(16):
                if n < 12 or (n - 12) // 2 == way:
                    sent(g.at[0, 0, 0], s_ring.at[way, n])

    @pl.when(c == 1)
    def _():
        sent(half0, s_a.at[0])
        for way in range(2):
            for n in range(16):
                if n < 8 or n % 2 == way:
                    sent(g.at[0, 0, 0], s_ring.at[way, n])


def local(jacobian, obs_weight, row_counts, tile_lists, tile_slot, probe_block):
    smem, vmem, hbm = (pl.BlockSpec(memory_space=m) for m in (pltpu.SMEM, pltpu.VMEM, pl.ANY))
    dma = lambda *shape: pltpu.SemaphoreType.DMA(shape)
    return pl.pallas_call(
        kernel,
        out_shape=jax.ShapeDtypeStruct((64, 64), BF16),
        in_specs=[smem, smem, smem, vmem, hbm, hbm],
        out_specs=vmem,
        scratch_shapes=[
            pltpu.SMEM((4, 16), jnp.int32),
            pltpu.VMEM((64, 256), BF16),
            pltpu.VMEM((8, 1024, 256), BF16),
            pltpu.VMEM((2, Z, X, 128, 128), BF16),
            pltpu.VMEM((256, 1024), BF16),
            pltpu.VMEM((8, 2, 4, 32, 128), F32),
            pltpu.VMEM((8, 2, 4, 32, 128), BF16),
            pltpu.VMEM((8, 2, 4, 32, 128), BF16),
            pltpu.VMEM((4, 4, 8, 32, 128), BF16),
            pltpu.VMEM((2, 2, 8, 32, 128), BF16),
            pltpu.VMEM((2, 2, 8, 32, 128), BF16),
            pltpu.VMEM((2, 2, 8, 32, 128), BF16),
            pltpu.VMEM((4, 8, 32, 128), BF16),
            pltpu.VMEM((6, 4, 32, 128), BF16),
            pltpu.VMEM((16, 32, 128), F32),
            dma(3), dma(8), dma(4), dma(8), dma(8), dma(16), dma(2, 16), dma(2, 16), dma(32), dma(32), dma(8), dma(8),
            dma(12), dma(12), dma(8), dma(8),
        ],
        compiler_params=pltpu.CompilerParams(collective_id=0, has_side_effects=True, vmem_limit_bytes=60 * 1024 * 1024),
    )(tile_lists.T, tile_slot, row_counts, obs_weight.reshape(8, 128), jacobian, probe_block)


def solution(mesh):
    placed = (P(("obs", "sub"), None), P(("obs", "sub")), P("obs"), P(), P(), P("obs", None))
    return jax.shard_map(local, mesh=mesh, in_specs=placed, out_specs=P("obs", "sub"), check_vma=False)
```

```python
import jax
import jax.numpy as jnp
from jax import lax
from jax.experimental import pallas as pl
from jax.experimental.pallas import tpu as pltpu
from jax.sharding import PartitionSpec as P

MESH = pl.DeviceIdType.MESH
X, Y, Z = 4, 4, 8
F32, BF16 = jnp.float32, jnp.bfloat16
NEAR = (1, 7, 2, 6, 3, 5, 4)
FAR = (4, 3, 5, 2, 6, 1, 7)


def kernel(lists_hbm, slot_hbm, count_hbm, w_hbm, jac_ref, probe_ref, out_ref,
           lists_ref, slot_ref, count_ref, table, w_ref, jv, g, img, cown, csend, crecv, d, r1, e, r2, fin, r3,
           s_in, s_jac, s_gz, r_gz, s_gx, r_gx, s_gp, r_gp, s_gb, r_gb, s_gq, r_gq, s_c, r_c, s_1, r_1, s_2, r_2, s_3, r_3):
    obs, y = lax.axis_index("obs"), lax.axis_index("sub")
    c = obs % 2
    x = (obs // 2) % X
    z = obs // (2 * X)

    def dev(zz, xx, cc):
        return ((zz * X + xx) * 2 + cc, y)

    partner = dev(z, x, 1 - c)
    role = 1 - c
    log = [[]]

    def remote(src, dst, s, r, to):
        return pltpu.make_async_remote_copy(src_ref=src, dst_ref=dst, send_sem=s, recv_sem=r, device_id=to, device_id_type=MESH)

    def send(src, dst, s, r, to):
        copy = remote(src, dst, s, r, to)
        copy.start()
        log[-1].append(copy)

    def arrived(dst, r):
        remote(dst, dst, s_in.at[0], r, partner).wait_recv()

    mine = g.at[z, x, c]
    inputs = [pltpu.make_async_copy(src, dst, s_in.at[i]) for i, (src, dst) in enumerate(
        ((probe_ref, mine), (lists_hbm, lists_ref), (slot_hbm, slot_ref), (count_hbm, count_ref), (w_hbm, w_ref)))]
    for copy in inputs:
        copy.start()
    jacs = [pltpu.make_async_copy(jac_ref.at[:, pl.ds(k * 256, 256)], jv.at[k], s_jac.at[k]) for k in range(8)]
    for copy in jacs:
        copy.start()

    def along(axis, by):
        dx = jnp.where(role == axis, 0, by)
        dy = jnp.where(role == axis, by, 0)
        return ((z * X + (x + dx) % X) * 2 + c, (y + dy) % Y)

    first = jnp.where(role == 0, y, x)
    second = jnp.where(role == 0, x, y)

    barrier = pltpu.get_barrier_semaphore()
    others = [dev((z + dz) % Z, x, c) for dz in range(1, Z)] + [partner]
    others += [along(axis, by) for axis in range(2) for by in range(1, 4)]
    for o in others:
        pl.semaphore_signal(barrier, inc=1, device_id=o, device_id_type=MESH)
    inputs[0].wait()
    pl.semaphore_wait(barrier, len(others))

    xo = (x + 2) % X

    def source(n):
        return (z + Z - ((0,) + NEAR)[n]) % Z

    def top(zz, xx):
        return g.at[zz, xx, c, pl.ds(0, 32)]

    def bottom(zz, xx):
        return g.at[zz, xx, c, pl.ds(32, 32)]

    def along_x(dx, zz, xx, n):
        return top(zz, xx) if dx == 2 and n else g.at[zz, xx, c]

    for dz in NEAR:
        send(mine, mine, s_gz.at[dz], r_gz.at[dz], dev((z + dz) % Z, x, c))

    def spread(n):
        zz = source(n)
        for dx in (1, 3, 2):
            q = along_x(dx, zz, x, n)
            send(q, q, s_gx.at[dx, n], r_gx.at[dx, n], dev(z, (x + dx) % X, c))
        q = g.at[zz, x, c]
        send(q, q, s_gp.at[0, n], r_gp.at[0, n], partner)

    spread(0)

    for n in range(1, 8):
        if n == 4:
            q = g.at[z, xo, c]
            arrived(q, r_gx.at[2, 0])
            for dz in NEAR:
                send(bottom(z, xo), bottom(z, xo), s_gb.at[dz], r_gb.at[dz], dev((z + dz) % Z, x, c))
            send(q, q, s_gp.at[2, 0], r_gp.at[2, 0], partner)
        arrived(g.at[source(n), x, c], r_gz.at[NEAR[n - 1]])
        spread(n)
    for n in range(8):
        zz = source(n)
        for dx in (1, 3, 2) if n else (1, 3):
            q = along_x(dx, zz, (x + X - dx) % X, n)
            arrived(q, r_gx.at[dx, n])
            send(q, q, s_gp.at[dx, n], r_gp.at[dx, n], partner)
        if n:
            q = bottom(zz, xo)
            arrived(q, r_gb.at[NEAR[n - 1]])
            send(q, q, s_gq.at[n], r_gq.at[n], partner)
    for copy in inputs[1:]:
        copy.wait()

    def fill(t, _):
        for which, owner in enumerate((obs, obs + 1 - 2 * c)):
            at, found = jnp.int32(0), jnp.int32(0)
            for k in range(8):
                hit = slot_ref[lists_ref[k, owner]] == t
                at = jnp.where(hit, k, at)
                found = jnp.where(hit, 1, found)
            table[2 * which, t] = at
            table[2 * which + 1, t] = found
        return 0

    lax.fori_loop(0, 16, fill, 0)

    for copy in jacs:
        copy.wait()
    for n in range(8):
        for dx in (0, 1, 3, 2):
            arrived(along_x(dx, z, x, n), r_gp.at[dx, n])
        if n:
            arrived(bottom(z, x), r_gq.at[n])

    def image(i, _):
        rows = pl.ds(pl.multiple_of(i * 256, 256), 256)
        total = jnp.zeros((256, 256), F32)
        for k in range(8):
            t = lists_ref[k, obs]
            cols = g[t // 2, pl.ds((t % 2) * 2, 2)].reshape(256, 256)
            total += jnp.dot(jv[k, rows, :], cols, preferred_element_type=F32)
        turned = total.T
        for j in range(2):
            lane = lax.broadcasted_iota(jnp.int32, (1, 128), 1) + (y * 1024 + (i * 2 + j) * 128)
            weight = jnp.where(lane < count_ref[0], w_ref[pl.ds(i * 2 + j, 1), :], 0.0)
            img[:, pl.ds(pl.multiple_of(i * 256 + j * 128, 128), 128)] = (turned[:, j * 128:(j + 1) * 128] * weight).astype(BF16)
        return 0

    lax.fori_loop(0, 4, image, 0, unroll=2)

    low = lax.broadcasted_iota(jnp.int32, (1, 1, 128), 2) < 64

    def contribution(k, _):
        total = jnp.dot(img[...], jv[k], preferred_element_type=F32).reshape(4, 2, 32, 256)
        for b in range(2):
            up = total[:, 0, :, b * 128:(b + 1) * 128]
            down = total[:, 1, :, b * 128:(b + 1) * 128]
            one = jnp.where(low, up, pltpu.roll(down, 64, 2))
            two = jnp.where(low, pltpu.roll(up, 64, 2), down)
            cown[k, b] = jnp.where(c == 0, one, two)
            csend[k, b] = jnp.where(c == 0, two, one).astype(BF16)
        remote(csend.at[k], crecv.at[k], s_c.at[k], r_c.at[k], partner).start()
        return 0

    lax.fori_loop(0, 8, contribution, 0)
    for k in range(8):
        arrived(crecv.at[k], r_c.at[k])

    def chip_sum(t, part):
        own = cown[(table[0, t],) + part] * table[1, t].astype(F32)
        other = crecv[(table[2, t],) + part].astype(F32) * table[3, t].astype(F32)
        return (own + other).astype(BF16)

    gathered = log[-1]
    log.append([])

    for by2 in (2, 1, 3, 0):
        s = (second + by2) % 4

        @pl.when(role == 0)
        def _():
            def place(zz, _):
                d[:, s, zz] = chip_sum(2 * zz + s // 2, (s % 2,))
                return 0

            lax.fori_loop(0, 8, place, 0)

        @pl.when(role == 1)
        def _():
            def place(t, _):
                both = chip_sum(t, (slice(None), s))
                for b in range(2):
                    d[2 * (t % 2) + b, s, t // 2] = both[b]
                return 0

            lax.fori_loop(0, 16, place, 0)

        for by in (2, 1, 3):
            send(d.at[(first + by) % 4, s], r1.at[by, by2], s_1.at[by, by2], r_1.at[by, by2], along(0, by))

    for copy in gathered:
        copy.wait_send()
    for k in range(8):
        remote(csend.at[k], crecv.at[k], s_c.at[k], r_c.at[k], partner).wait_send()

    for by2 in (2, 1, 3, 0):
        s = (second + by2) % 4
        for by in (1, 3, 2):
            arrived(r1.at[by, by2], r_1.at[by, by2])
        total = d[first, s].astype(F32) + r1[1, by2].astype(F32) + r1[3, by2].astype(F32) + r1[2, by2].astype(F32)
        if by2:
            e[by2] = total.astype(BF16)
        else:
            fin[...] = total
        if by2:
            send(e.at[by2], r2.at[by2], s_2.at[by2], r_2.at[by2], along(1, by2))
    for by2 in (1, 3, 2):
        arrived(r2.at[by2], r_2.at[by2])

    for dz in FAR:
        zz = (z + dz) % Z
        fin[zz] = fin[zz] + r2[1, zz].astype(F32) + r2[3, zz].astype(F32) + r2[2, zz].astype(F32)
        send(fin.at[zz], r3.at[dz], s_3.at[dz], r_3.at[dz], dev(zz, x, c))
    total = fin[z] + r2[1, z].astype(F32) + r2[3, z].astype(F32) + r2[2, z].astype(F32)
    for dz in NEAR:
        arrived(r3.at[dz], r_3.at[dz])
        total = total + r3[dz]
    turned = total.T
    out_ref[:, 0:32] = turned[0:64].astype(BF16)
    out_ref[:, 32:64] = turned[64:128].astype(BF16)

    for copy in log[-1]:
        copy.wait_send()


def local(jacobian, obs_weight, row_counts, tile_lists, tile_slot, probe_block):
    dma = lambda *shape: pltpu.SemaphoreType.DMA(shape)
    return pl.pallas_call(
        kernel,
        out_shape=jax.ShapeDtypeStruct((64, 64), BF16),
        in_specs=[pl.BlockSpec(memory_space=pl.ANY)] * 6,
        out_specs=pl.BlockSpec(memory_space=pltpu.VMEM),
        scratch_shapes=[
            pltpu.SMEM((8, 64), jnp.int32),
            pltpu.SMEM((16,), jnp.int32),
            pltpu.SMEM((1,), jnp.int32),
            pltpu.SMEM((4, 16), jnp.int32),
            pltpu.VMEM((8, 128), F32),
            pltpu.VMEM((8, 1024, 256), BF16),
            pltpu.VMEM((Z, X, 2, 64, 256), BF16),
            pltpu.VMEM((256, 1024), BF16),
            pltpu.VMEM((8, 2, 4, 32, 128), F32),
            pltpu.VMEM((8, 2, 4, 32, 128), BF16),
            pltpu.VMEM((8, 2, 4, 32, 128), BF16),
            pltpu.VMEM((4, 4, 8, 32, 128), BF16),
            pltpu.VMEM((4, 4, 8, 32, 128), BF16),
            pltpu.VMEM((4, 8, 32, 128), BF16),
            pltpu.VMEM((4, 8, 32, 128), BF16),
            pltpu.VMEM((8, 32, 128), F32),
            pltpu.VMEM((8, 32, 128), F32),
            dma(5), dma(8), dma(8), dma(8), dma(4, 8), dma(4, 8), dma(4, 8), dma(4, 8),
            dma(8), dma(8), dma(8), dma(8), dma(8), dma(8),
            dma(4, 4), dma(4, 4), dma(4), dma(4), dma(8), dma(8),
        ],
        compiler_params=pltpu.CompilerParams(collective_id=0, has_side_effects=True, vmem_limit_bytes=60 * 1024 * 1024),
    )(tile_lists.T, tile_slot, row_counts, obs_weight.reshape(8, 128), jacobian, probe_block)


def solution(mesh):
    placed = (P(("obs", "sub"), None), P(("obs", "sub")), P("obs"), P(), P(), P("obs", None))
    return jax.shard_map(local, mesh=mesh, in_specs=placed, out_specs=P("obs", "sub"), check_vma=False)
```

```python
import jax
import jax.numpy as jnp
from jax import lax
from jax.experimental import pallas as pl
from jax.experimental.pallas import tpu as pltpu
from jax.sharding import PartitionSpec as P

MESH = pl.DeviceIdType.MESH
X, Y, Z = 4, 4, 8
F32, BF16 = jnp.float32, jnp.bfloat16
NEAR = (1, 7, 2, 6, 3, 5, 4)
FAR = (4, 3, 5, 2, 6, 1, 7)
TURNED = (1, 2, 3, 4)


def kernel(lists_hbm, slot_hbm, count_hbm, w_hbm, jac_ref, probe_ref, out_ref,
           lists_ref, slot_ref, count_ref, table, w_ref, jv, g, img, cown, csend, crecv, d, r1, e, r2, fin, fout, r3, ro, so, rf,
           s_in, s_jac, s_gz, r_gz, s_gx, r_gx, s_gp, r_gp, s_go, r_go, s_c, r_c, s_1, r_1, s_2, r_2, s_3, r_3, s_o, r_o, s_f, r_f):
    obs, y = lax.axis_index("obs"), lax.axis_index("sub")
    c = obs % 2
    x = (obs // 2) % X
    z = obs // (2 * X)

    def dev(zz, xx, cc):
        return ((zz * X + xx) * 2 + cc, y)

    partner = dev(z, x, 1 - c)
    role = 1 - c
    log = [[]]

    def remote(src, dst, s, r, to):
        return pltpu.make_async_remote_copy(src_ref=src, dst_ref=dst, send_sem=s, recv_sem=r, device_id=to, device_id_type=MESH)

    def send(src, dst, s, r, to):
        copy = remote(src, dst, s, r, to)
        copy.start()
        log[-1].append(copy)

    def arrived(dst, r):
        remote(dst, dst, s_in.at[0], r, partner).wait_recv()

    mine = g.at[z, x, c]
    inputs = [pltpu.make_async_copy(src, dst, s_in.at[i]) for i, (src, dst) in enumerate(
        ((probe_ref, mine), (lists_hbm, lists_ref), (slot_hbm, slot_ref), (count_hbm, count_ref), (w_hbm, w_ref)))]
    for copy in inputs:
        copy.start()
    jacs = [pltpu.make_async_copy(jac_ref.at[:, pl.ds(k * 256, 256)], jv.at[k], s_jac.at[k]) for k in range(8)]
    for copy in jacs:
        copy.start()

    def along(axis, by):
        return at(by, 0) if axis == 0 else at(0, by)

    def at(by, by2):
        dx = jnp.where(role == 0, by2, by)
        dy = jnp.where(role == 0, by, by2)
        return ((z * X + (x + dx) % X) * 2 + c, (y + dy) % Y)

    first = jnp.where(role == 0, y, x)
    second = jnp.where(role == 0, x, y)

    barrier = pltpu.get_barrier_semaphore()
    others = [dev((z + dz) % Z, x, c) for dz in range(1, Z)] + [partner]
    others += [along(axis, by) for axis in range(2) for by in range(1, 4)] + [at(2, by2) for by2 in range(1, 4)]
    for o in others:
        pl.semaphore_signal(barrier, inc=1, device_id=o, device_id_type=MESH)
    inputs[0].wait()
    pl.semaphore_wait(barrier, len(others))

    xo = (x + 2) % X

    def source(n):
        return (z + Z - ((0,) + NEAR)[n]) % Z

    def hand_over(dx, n, r):
        q = g.at[source(n), (x + X - dx) % X, c]
        arrived(q, r)
        send(q, q, s_gp.at[dx, n], r_gp.at[dx, n], partner)

    def spread(n):
        q = g.at[source(n), x, c]
        for dx in (1, 3) if n in TURNED else (1, 3, 2):
            send(q, q, s_gx.at[dx, n], r_gx.at[dx, n], dev(z, (x + dx) % X, c))
        send(q, q, s_gp.at[0, n], r_gp.at[0, n], partner)

    for dz in NEAR:
        send(mine, mine, s_gz.at[dz], r_gz.at[dz], dev((z + dz) % Z, x, c))
    spread(0)
    for n in range(1, 8):
        if n == 4:
            q = g.at[z, xo, c]
            arrived(q, r_gx.at[2, 0])
            for dz in [NEAR[i - 1] for i in TURNED]:
                send(q, q, s_go.at[dz], r_go.at[dz], dev((z + dz) % Z, x, c))
            send(q, q, s_gp.at[2, 0], r_gp.at[2, 0], partner)
        if n == 3:
            for dx in (1, 3):
                hand_over(dx, 0, r_gx.at[dx, 0])
        arrived(g.at[source(n), x, c], r_gz.at[NEAR[n - 1]])
        spread(n)
    for n in range(1, 8):
        for dx in (1, 3):
            hand_over(dx, n, r_gx.at[dx, n])
        hand_over(2, n, r_go.at[NEAR[n - 1]] if n in TURNED else r_gx.at[2, n])
    for copy in inputs[1:]:
        copy.wait()

    def fill(t, _):
        for which, owner in enumerate((obs, obs + 1 - 2 * c)):
            at, found = jnp.int32(0), jnp.int32(0)
            for k in range(8):
                hit = slot_ref[lists_ref[k, owner]] == t
                at = jnp.where(hit, k, at)
                found = jnp.where(hit, 1, found)
            table[2 * which, t] = at
            table[2 * which + 1, t] = found
        return 0

    lax.fori_loop(0, 16, fill, 0)

    for copy in jacs:
        copy.wait()
    for n in range(8):
        for dx in (0, 1, 3, 2):
            arrived(mine, r_gp.at[dx, n])

    def image(i, _):
        rows = pl.ds(pl.multiple_of(i * 256, 256), 256)
        total = jnp.zeros((256, 256), F32)
        for k in range(8):
            t = lists_ref[k, obs]
            cols = g[t // 2, pl.ds((t % 2) * 2, 2)].reshape(256, 256)
            total += jnp.dot(jv[k, rows, :], cols, preferred_element_type=F32)
        turned = total.T
        for j in range(2):
            lane = lax.broadcasted_iota(jnp.int32, (1, 128), 1) + (y * 1024 + (i * 2 + j) * 128)
            weight = jnp.where(lane < count_ref[0], w_ref[pl.ds(i * 2 + j, 1), :], 0.0)
            img[:, pl.ds(pl.multiple_of(i * 256 + j * 128, 128), 128)] = (turned[:, j * 128:(j + 1) * 128] * weight).astype(BF16)
        return 0

    lax.fori_loop(0, 4, image, 0, unroll=2)

    low = lax.broadcasted_iota(jnp.int32, (1, 1, 128), 2) < 64

    def contribution(k, _):
        total = jnp.dot(img[...], jv[k], preferred_element_type=F32).reshape(4, 2, 32, 256)
        for b in range(2):
            up = total[:, 0, :, b * 128:(b + 1) * 128]
            down = total[:, 1, :, b * 128:(b + 1) * 128]
            one = jnp.where(low, up, pltpu.roll(down, 64, 2))
            two = jnp.where(low, pltpu.roll(up, 64, 2), down)
            cown[k, b] = jnp.where(c == 0, one, two)
            csend[k, b] = jnp.where(c == 0, two, one).astype(BF16)
        remote(csend.at[k], crecv.at[k], s_c.at[k], r_c.at[k], partner).start()
        return 0

    lax.fori_loop(0, 8, contribution, 0)
    for k in range(8):
        arrived(crecv.at[k], r_c.at[k])

    def chip_sum(t, part):
        own = cown[(table[0, t],) + part] * table[1, t].astype(F32)
        other = crecv[(table[2, t],) + part].astype(F32) * table[3, t].astype(F32)
        return (own + other).astype(BF16)

    gathered = log[-1]
    log.append([])

    for by2 in (2, 1, 3, 0):
        s = (second + by2) % 4

        @pl.when(role == 0)
        def _():
            def place(zz, _):
                d[:, s, zz] = chip_sum(2 * zz + s // 2, (s % 2,))
                return 0

            lax.fori_loop(0, 8, place, 0)

        @pl.when(role == 1)
        def _():
            def place(t, _):
                both = chip_sum(t, (slice(None), s))
                for b in range(2):
                    d[2 * (t % 2) + b, s, t // 2] = both[b]
                return 0

            lax.fori_loop(0, 16, place, 0)

        for by in (1, 3):
            send(d.at[(first + by) % 4, s], r1.at[by, by2], s_1.at[by, by2], r_1.at[by, by2], along(0, by))

    opposite = (first + 2) % 4
    for dz in NEAR:
        send(d.at[opposite, :, (z + dz) % Z], ro.at[dz], s_o.at[dz], r_o.at[dz], dev((z + dz) % Z, x, c))

    for copy in gathered:
        copy.wait_send()
    for k in range(8):
        remote(csend.at[k], crecv.at[k], s_c.at[k], r_c.at[k], partner).wait_send()

    for by2 in (2, 1, 3, 0):
        s = (second + by2) % 4
        for by in (1, 3):
            arrived(r1.at[by, by2], r_1.at[by, by2])
        total = d[first, s].astype(F32) + r1[1, by2].astype(F32) + r1[3, by2].astype(F32)
        if by2:
            e[by2] = total.astype(BF16)
        else:
            fin[...] = total
        if by2:
            send(e.at[by2], r2.at[by2], s_2.at[by2], r_2.at[by2], along(1, by2))
    for by2 in (1, 3, 2):
        arrived(r2.at[by2], r_2.at[by2])

    for dz in FAR:
        zz = (z + dz) % Z
        total = fin[zz] + r2[1, zz].astype(F32) + r2[3, zz].astype(F32) + r2[2, zz].astype(F32)
        fout[dz] = total.astype(BF16)
        send(fout.at[dz], r3.at[dz], s_3.at[dz], r_3.at[dz], dev(zz, x, c))
    total = fin[z] + r2[1, z].astype(F32) + r2[3, z].astype(F32) + r2[2, z].astype(F32)
    across = d[opposite, :, z].astype(F32)
    for dz in NEAR:
        arrived(ro.at[dz], r_o.at[dz])
        across = across + ro[dz].astype(F32)
    so[...] = across
    for by2 in (2, 1, 3, 0):
        send(so.at[(second + by2) % 4], rf.at[by2], s_f.at[by2], r_f.at[by2], at(2, by2))
    for dz in NEAR:
        arrived(r3.at[dz], r_3.at[dz])
        total = total + r3[dz].astype(F32)
    for by2 in (0, 1, 3, 2):
        arrived(rf.at[by2], r_f.at[by2])
        total = total + rf[by2]
    turned = total.T
    out_ref[:, 0:32] = turned[0:64].astype(BF16)
    out_ref[:, 32:64] = turned[64:128].astype(BF16)

    for copy in log[-1]:
        copy.wait_send()


def local(jacobian, obs_weight, row_counts, tile_lists, tile_slot, probe_block):
    dma = lambda *shape: pltpu.SemaphoreType.DMA(shape)
    return pl.pallas_call(
        kernel,
        out_shape=jax.ShapeDtypeStruct((64, 64), BF16),
        in_specs=[pl.BlockSpec(memory_space=pl.ANY)] * 6,
        out_specs=pl.BlockSpec(memory_space=pltpu.VMEM),
        scratch_shapes=[
            pltpu.SMEM((8, 64), jnp.int32),
            pltpu.SMEM((16,), jnp.int32),
            pltpu.SMEM((1,), jnp.int32),
            pltpu.SMEM((4, 16), jnp.int32),
            pltpu.VMEM((8, 128), F32),
            pltpu.VMEM((8, 1024, 256), BF16),
            pltpu.VMEM((Z, X, 2, 64, 256), BF16),
            pltpu.VMEM((256, 1024), BF16),
            pltpu.VMEM((8, 2, 4, 32, 128), F32),
            pltpu.VMEM((8, 2, 4, 32, 128), BF16),
            pltpu.VMEM((8, 2, 4, 32, 128), BF16),
            pltpu.VMEM((4, 4, 8, 32, 128), BF16),
            pltpu.VMEM((4, 4, 8, 32, 128), BF16),
            pltpu.VMEM((4, 8, 32, 128), BF16),
            pltpu.VMEM((4, 8, 32, 128), BF16),
            pltpu.VMEM((8, 32, 128), F32),
            pltpu.VMEM((8, 32, 128), BF16),
            pltpu.VMEM((8, 32, 128), BF16),
            pltpu.VMEM((8, 4, 32, 128), BF16),
            pltpu.VMEM((4, 32, 128), F32),
            pltpu.VMEM((4, 32, 128), F32),
            dma(5), dma(8), dma(8), dma(8), dma(4, 8), dma(4, 8), dma(4, 8), dma(4, 8),
            dma(8), dma(8), dma(8), dma(8),
            dma(4, 4), dma(4, 4), dma(4), dma(4), dma(8), dma(8), dma(8), dma(8), dma(4), dma(4),
        ],
        compiler_params=pltpu.CompilerParams(collective_id=0, has_side_effects=True, vmem_limit_bytes=60 * 1024 * 1024),
    )(tile_lists.T, tile_slot, row_counts, obs_weight.reshape(8, 128), jacobian, probe_block)


def solution(mesh):
    placed = (P(("obs", "sub"), None), P(("obs", "sub")), P("obs"), P(), P(), P("obs", None))
    return jax.shard_map(local, mesh=mesh, in_specs=placed, out_specs=P("obs", "sub"), check_vma=False)
```

```python
import jax
import jax.numpy as jnp
from jax import lax
from jax.experimental import pallas as pl
from jax.experimental.pallas import tpu as pltpu
from jax.sharding import PartitionSpec as P

MESH = pl.DeviceIdType.MESH
X, Y, Z = 4, 4, 8
F32, BF16 = jnp.float32, jnp.bfloat16
NEAR = (1, 7, 2, 6, 3, 5, 4)
FAR = (4, 3, 5, 2, 6, 1, 7)
TURNED = (1, 2)


def kernel(lists_hbm, slot_hbm, count_hbm, w_hbm, jac_ref, probe_ref, out_ref,
           lists_ref, slot_ref, count_ref, table, w_ref, jv, g, img, cown, csend, crecv, d, r1, e, r2, fin, fout, r3, ro, so, rf,
           s_in, s_jac, s_gz, r_gz, s_gx, r_gx, s_gp, r_gp, s_go, r_go, s_c, r_c, s_1, r_1, s_2, r_2, s_3, r_3, s_o, r_o, s_f, r_f):
    obs, y = lax.axis_index("obs"), lax.axis_index("sub")
    c = obs % 2
    x = (obs // 2) % X
    z = obs // (2 * X)

    def dev(zz, xx, cc):
        return ((zz * X + xx) * 2 + cc, y)

    partner = dev(z, x, 1 - c)
    role = 1 - c
    log = [[]]

    def remote(src, dst, s, r, to):
        return pltpu.make_async_remote_copy(src_ref=src, dst_ref=dst, send_sem=s, recv_sem=r, device_id=to, device_id_type=MESH)

    def send(src, dst, s, r, to):
        copy = remote(src, dst, s, r, to)
        copy.start()
        log[-1].append(copy)

    def arrived(dst, r):
        remote(dst, dst, s_in.at[0], r, partner).wait_recv()

    mine = g.at[z, x, c]
    inputs = [pltpu.make_async_copy(src, dst, s_in.at[i]) for i, (src, dst) in enumerate(
        ((probe_ref, mine), (lists_hbm, lists_ref), (slot_hbm, slot_ref), (count_hbm, count_ref), (w_hbm, w_ref)))]
    for copy in inputs:
        copy.start()
    jacs = [pltpu.make_async_copy(jac_ref.at[:, pl.ds(k * 256, 256)], jv.at[k], s_jac.at[k]) for k in range(8)]
    for copy in jacs:
        copy.start()

    def along(axis, by):
        return at(by, 0) if axis == 0 else at(0, by)

    def at(by, by2):
        dx = jnp.where(role == 0, by2, by)
        dy = jnp.where(role == 0, by, by2)
        return ((z * X + (x + dx) % X) * 2 + c, (y + dy) % Y)

    first = jnp.where(role == 0, y, x)
    second = jnp.where(role == 0, x, y)

    barrier = pltpu.get_barrier_semaphore()
    others = [dev((z + dz) % Z, x, c) for dz in range(1, Z)] + [partner]
    others += [along(axis, by) for axis in range(2) for by in range(1, 4)] + [at(2, by2) for by2 in range(1, 4)]
    for o in others:
        pl.semaphore_signal(barrier, inc=1, device_id=o, device_id_type=MESH)
    inputs[0].wait()
    pl.semaphore_wait(barrier, len(others))

    xo = (x + 2) % X

    def source(n):
        return (z + Z - ((0,) + NEAR)[n]) % Z

    def hand_over(dx, n, r):
        q = g.at[source(n), (x + X - dx) % X, c]
        arrived(q, r)
        send(q, q, s_gp.at[dx, n], r_gp.at[dx, n], partner)

    def spread(n):
        q = g.at[source(n), x, c]
        for dx in (1, 3) if n in TURNED else (1, 3, 2):
            send(q, q, s_gx.at[dx, n], r_gx.at[dx, n], dev(z, (x + dx) % X, c))
        send(q, q, s_gp.at[0, n], r_gp.at[0, n], partner)

    for dz in NEAR:
        send(mine, mine, s_gz.at[dz], r_gz.at[dz], dev((z + dz) % Z, x, c))
    spread(0)
    for n in range(1, 8):
        if n == 4:
            q = g.at[z, xo, c]
            arrived(q, r_gx.at[2, 0])
            for dz in [NEAR[i - 1] for i in TURNED]:
                send(q, q, s_go.at[dz], r_go.at[dz], dev((z + dz) % Z, x, c))
            send(q, q, s_gp.at[2, 0], r_gp.at[2, 0], partner)
        if n == 3:
            for dx in (1, 3):
                hand_over(dx, 0, r_gx.at[dx, 0])
        arrived(g.at[source(n), x, c], r_gz.at[NEAR[n - 1]])
        spread(n)
    for n in range(1, 8):
        for dx in (1, 3):
            hand_over(dx, n, r_gx.at[dx, n])
        hand_over(2, n, r_go.at[NEAR[n - 1]] if n in TURNED else r_gx.at[2, n])
    for copy in inputs[1:]:
        copy.wait()

    def fill(t, _):
        for which, owner in enumerate((obs, obs + 1 - 2 * c)):
            at, found = jnp.int32(0), jnp.int32(0)
            for k in range(8):
                hit = slot_ref[lists_ref[k, owner]] == t
                at = jnp.where(hit, k, at)
                found = jnp.where(hit, 1, found)
            table[2 * which, t] = at
            table[2 * which + 1, t] = found
        return 0

    lax.fori_loop(0, 16, fill, 0)

    for copy in jacs:
        copy.wait()
    for n in range(8):
        for dx in (0, 1, 3, 2):
            arrived(mine, r_gp.at[dx, n])

    def image(i, _):
        rows = pl.ds(pl.multiple_of(i * 256, 256), 256)
        total = jnp.zeros((256, 256), F32)
        for k in range(8):
            t = lists_ref[k, obs]
            cols = g[t // 2, pl.ds((t % 2) * 2, 2)].reshape(256, 256)
            total += jnp.dot(jv[k, rows, :], cols, preferred_element_type=F32)
        turned = total.T
        for j in range(2):
            lane = lax.broadcasted_iota(jnp.int32, (1, 128), 1) + (y * 1024 + (i * 2 + j) * 128)
            weight = jnp.where(lane < count_ref[0], w_ref[pl.ds(i * 2 + j, 1), :], 0.0)
            img[:, pl.ds(pl.multiple_of(i * 256 + j * 128, 128), 128)] = (turned[:, j * 128:(j + 1) * 128] * weight).astype(BF16)
        return 0

    lax.fori_loop(0, 4, image, 0, unroll=2)

    low = lax.broadcasted_iota(jnp.int32, (1, 1, 128), 2) < 64

    def contribution(k, _):
        total = jnp.dot(img[...], jv[k], preferred_element_type=F32).reshape(4, 2, 32, 256)
        for b in range(2):
            up = total[:, 0, :, b * 128:(b + 1) * 128]
            down = total[:, 1, :, b * 128:(b + 1) * 128]
            one = jnp.where(low, up, pltpu.roll(down, 64, 2))
            two = jnp.where(low, pltpu.roll(up, 64, 2), down)
            cown[k, b] = jnp.where(c == 0, one, two)
            csend[k, b] = jnp.where(c == 0, two, one).astype(BF16)
        remote(csend.at[k], crecv.at[k], s_c.at[k], r_c.at[k], partner).start()
        return 0

    lax.fori_loop(0, 8, contribution, 0)
    for k in range(8):
        arrived(crecv.at[k], r_c.at[k])

    def chip_sum(t, part):
        own = cown[(table[0, t],) + part] * table[1, t].astype(F32)
        other = crecv[(table[2, t],) + part].astype(F32) * table[3, t].astype(F32)
        return (own + other).astype(BF16)

    gathered = log[-1]
    log.append([])

    for by2 in (2, 1, 3, 0):
        s = (second + by2) % 4

        @pl.when(role == 0)
        def _():
            def place(zz, _):
                d[:, s, zz] = chip_sum(2 * zz + s // 2, (s % 2,))
                return 0

            lax.fori_loop(0, 8, place, 0)

        @pl.when(role == 1)
        def _():
            def place(t, _):
                both = chip_sum(t, (slice(None), s))
                for b in range(2):
                    d[2 * (t % 2) + b, s, t // 2] = both[b]
                return 0

            lax.fori_loop(0, 16, place, 0)

        for by in (1, 3):
            send(d.at[(first + by) % 4, s], r1.at[by, by2], s_1.at[by, by2], r_1.at[by, by2], along(0, by))

    opposite = (first + 2) % 4
    for dz in NEAR:
        send(d.at[opposite, :, (z + dz) % Z], ro.at[dz], s_o.at[dz], r_o.at[dz], dev((z + dz) % Z, x, c))

    for copy in gathered:
        copy.wait_send()
    for k in range(8):
        remote(csend.at[k], crecv.at[k], s_c.at[k], r_c.at[k], partner).wait_send()

    for by2 in (2, 1, 3, 0):
        s = (second + by2) % 4
        for by in (1, 3):
            arrived(r1.at[by, by2], r_1.at[by, by2])
        total = d[first, s].astype(F32) + r1[1, by2].astype(F32) + r1[3, by2].astype(F32)
        if by2:
            e[by2] = total.astype(BF16)
        else:
            fin[...] = total
        if by2:
            send(e.at[by2], r2.at[by2], s_2.at[by2], r_2.at[by2], along(1, by2))
    for by2 in (1, 3, 2):
        arrived(r2.at[by2], r_2.at[by2])

    for dz in FAR:
        zz = (z + dz) % Z
        total = fin[zz] + r2[1, zz].astype(F32) + r2[3, zz].astype(F32) + r2[2, zz].astype(F32)
        fout[dz] = total.astype(BF16)
        send(fout.at[dz], r3.at[dz], s_3.at[dz], r_3.at[dz], dev(zz, x, c))
    total = fin[z] + r2[1, z].astype(F32) + r2[3, z].astype(F32) + r2[2, z].astype(F32)
    across = d[opposite, :, z].astype(F32)
    for dz in NEAR:
        arrived(ro.at[dz], r_o.at[dz])
        across = across + ro[dz].astype(F32)
    so[...] = across.astype(BF16)
    for by2 in (2, 1, 3, 0):
        send(so.at[(second + by2) % 4], rf.at[by2], s_f.at[by2], r_f.at[by2], at(2, by2))
    for dz in NEAR:
        arrived(r3.at[dz], r_3.at[dz])
        total = total + r3[dz].astype(F32)
    for by2 in (0, 1, 3, 2):
        arrived(rf.at[by2], r_f.at[by2])
        total = total + rf[by2].astype(F32)
    turned = total.T
    out_ref[:, 0:32] = turned[0:64].astype(BF16)
    out_ref[:, 32:64] = turned[64:128].astype(BF16)

    for copy in log[-1]:
        copy.wait_send()


def local(jacobian, obs_weight, row_counts, tile_lists, tile_slot, probe_block):
    dma = lambda *shape: pltpu.SemaphoreType.DMA(shape)
    return pl.pallas_call(
        kernel,
        out_shape=jax.ShapeDtypeStruct((64, 64), BF16),
        in_specs=[pl.BlockSpec(memory_space=pl.ANY)] * 6,
        out_specs=pl.BlockSpec(memory_space=pltpu.VMEM),
        scratch_shapes=[
            pltpu.SMEM((8, 64), jnp.int32),
            pltpu.SMEM((16,), jnp.int32),
            pltpu.SMEM((1,), jnp.int32),
            pltpu.SMEM((4, 16), jnp.int32),
            pltpu.VMEM((8, 128), F32),
            pltpu.VMEM((8, 1024, 256), BF16),
            pltpu.VMEM((Z, X, 2, 64, 256), BF16),
            pltpu.VMEM((256, 1024), BF16),
            pltpu.VMEM((8, 2, 4, 32, 128), F32),
            pltpu.VMEM((8, 2, 4, 32, 128), BF16),
            pltpu.VMEM((8, 2, 4, 32, 128), BF16),
            pltpu.VMEM((4, 4, 8, 32, 128), BF16),
            pltpu.VMEM((4, 4, 8, 32, 128), BF16),
            pltpu.VMEM((4, 8, 32, 128), BF16),
            pltpu.VMEM((4, 8, 32, 128), BF16),
            pltpu.VMEM((8, 32, 128), F32),
            pltpu.VMEM((8, 32, 128), BF16),
            pltpu.VMEM((8, 32, 128), BF16),
            pltpu.VMEM((8, 4, 32, 128), BF16),
            pltpu.VMEM((4, 32, 128), BF16),
            pltpu.VMEM((4, 32, 128), BF16),
            dma(5), dma(8), dma(8), dma(8), dma(4, 8), dma(4, 8), dma(4, 8), dma(4, 8),
            dma(8), dma(8), dma(8), dma(8),
            dma(4, 4), dma(4, 4), dma(4), dma(4), dma(8), dma(8), dma(8), dma(8), dma(4), dma(4),
        ],
        compiler_params=pltpu.CompilerParams(collective_id=0, has_side_effects=True, vmem_limit_bytes=60 * 1024 * 1024),
    )(tile_lists.T, tile_slot, row_counts, obs_weight.reshape(8, 128), jacobian, probe_block)


def solution(mesh):
    placed = (P(("obs", "sub"), None), P(("obs", "sub")), P("obs"), P(), P(), P("obs", None))
    return jax.shard_map(local, mesh=mesh, in_specs=placed, out_specs=P("obs", "sub"), check_vma=False)
```
